32 devices in a mesh: dp: 8 (over y, x, core), fsdp: 4 (over z).
Axes of the slice: x: 2, y: 2, z: 4, core: 2. Of those that a mesh axis runs over, the one named last changes fastest.
Arguments:
- tokens: bfloat16 [1024, 5120], P('dp'), may hold values from -6 to 6
- targets: bfloat16 [1024, 5120], P('dp'), may hold values from -12 to 12
- norm_gain: float32 [5120], replicated, may hold values from 0.5 to 1.5
- up_master: float32 [5120, 6912], P('dp', 'fsdp'), may hold values from -0.078125 to 0.078125
- down_master: float32 [6912, 5120], P('fsdp', 'dp'), may hold values from -0.078125 to 0.078125
- up_probe: int32 [160, 6912], P(None, 'fsdp'), may hold values from -2147483648 to 2147483646
- down_probe: int32 [6912, 160], P('fsdp'), may hold values from -2147483648 to 2147483646
- up_first: float32 [5120, 6912], P('dp', 'fsdp'), may hold values from -0.012 to 0.012
- up_second: float32 [5120, 6912], P('dp', 'fsdp'), may hold values from 0.0001 to 0.001
- down_first: float32 [6912, 5120], P('fsdp', 'dp'), may hold values from -0.012 to 0.012
- down_second: float32 [6912, 5120], P('fsdp', 'dp'), may hold values from 0.0001 to 0.001
Outputs:
- loss: float32 [], replicated
- up_moment: float32 [5120, 6912], P('dp', 'fsdp')
- up_curvature: float32 [5120, 6912], P('dp', 'fsdp')
- up_step: float32 [5120, 6912], P('dp', 'fsdp')
- down_moment: float32 [6912, 5120], P('fsdp', 'dp')
- down_curvature: float32 [6912, 5120], P('fsdp', 'dp')
- down_step: float32 [6912, 5120], P('fsdp', 'dp')
The draws below stay inside these ranges and needn't reach their ends.
Inputs may be any that keep to these rules, and one draw needn't show every extreme that they name: `up_probe`: any 32-bit word; each bit gives one probe sign. `down_probe`: any 32-bit word; each bit gives one probe sign.
All inputs are finite; a program needn't handle non-finite values.
Results may differ from the reference program's by a relative error of at most 0.03.
Values may be sent and summed in bfloat16 or wider, within the bound.
A program may use at most 320 MiB of HBM per device.

```python
import math
import jax
import jax.numpy as jnp
from jax import lax

D = 5120
FF = 6912
TOK_DEV = 128
BLOCK = 16
STEP = 10
TOKENS = 1024
N_DP = 8


def draw_targets(key, part):
    rows = jnp.arange(TOKENS, dtype=jnp.float32)[:, None]
    ratio = rows / jnp.float32(max(TOKENS - 1, 1))
    scale = jnp.exp(ratio * jnp.log(jnp.float32(3.0)))
    base = jnp.clip(jax.random.normal(key, (TOKENS, D), jnp.float32), -4.0, 4.0)
    return (base * scale).astype(jnp.bfloat16)


def with_ends(entries, own_key, low, largest):
    extent = entries.shape
    place = [jax.random.randint(jax.random.fold_in(own_key, axis), (), 0, extent[axis]) for axis in range(len(extent))]
    entries = entries.at[tuple(place)].set(low)
    longest = extent.index(max(extent))
    place[longest] = (place[longest] + 1) % extent[longest]
    return entries.at[tuple(place)].set(largest)


def with_spikes(values, stream_key, source, target, blocks, factor):
    def block_of(axis_at):
        return (jnp.arange(values.shape[axis_at]) // (values.shape[axis_at] // blocks)).reshape((-1,) + (1,) * (values.ndim - 1 - axis_at))

    near = jax.random.permutation(stream_key, blocks)[block_of(target)]
    second = (block_of(target) + blocks // 2) % blocks
    return jnp.where((block_of(source) == near) | (block_of(source) == second), factor * values, values)


def block_scale(key, shape, shards, low, top_value):
    def one(axis_at, blocks):
        heights = jax.random.uniform(jax.random.fold_in(jax.random.fold_in(key, 6), axis_at), (blocks,), jnp.float32, low / len(shards), top_value / len(shards))
        return jnp.repeat(jnp.exp(heights), shape[axis_at] // blocks).reshape((-1,) + (1,) * (len(shape) - axis_at - 1))

    level = one(*shards[0])
    for cut in shards[1:]:
        level = level * one(*cut)
    return level


def gaussian(own_key, extent, scale, bound, split=(), held_as=jnp.bfloat16):
    drawn = jax.random.normal(own_key, extent, jnp.float32) * scale
    if len(split) > 0:
        drawn = block_scale(own_key, extent, split, -0.22, 0.18) * drawn
    return jnp.clip(drawn, min=-bound, max=bound).astype(held_as)


def gaussian_with(stream_key, dims, width, limit, split, heavy, kind=jnp.bfloat16):
    drawn = width * jax.random.normal(stream_key, dims, jnp.float32)
    if split:
        drawn = drawn * block_scale(stream_key, dims, split, -0.22, 0.18)
    return jnp.clip(with_spikes(drawn, jax.random.fold_in(stream_key, 3), *heavy), -limit, limit).astype(kind)


def setup_inputs(seed: int = 0) -> dict:
    splits = jax.random.split(jax.random.key(seed), 12)
    tokens = gaussian_with(splits[0], (TOKENS, D), 1.0, 6.0, ((0, 8),), (0, 1, 8, 2.0))
    targets = draw_targets(jax.random.fold_in(splits[11], 71), 0)
    norm_gain = jnp.clip(1.0 + 0.1 * jax.random.normal(splits[2], (D,), jnp.float32), 0.5, 1.5)
    up_master = gaussian(splits[3], (D, FF), D ** -0.5, 0.078125, ((0, 8), (1, 4)), jnp.float32)
    down_master = gaussian(splits[4], (FF, D), FF ** -0.5, 0.078125, ((0, 4), (1, 8)), jnp.float32)
    up_probe = with_ends(jax.random.randint(splits[5], (D // 32, FF), -2147483648, 2147483647), jax.random.fold_in(splits[5], 1), -2147483648, 2147483646).astype(jnp.int32)
    down_probe = with_ends(jax.random.randint(splits[6], (FF, D // 32), -2147483648, 2147483647), jax.random.fold_in(splits[6], 1), -2147483648, 2147483646).astype(jnp.int32)
    up_first = gaussian(splits[7], (D, FF), 0.002, 0.012, ((0, 8), (1, 4)), jnp.float32)
    up_second = jnp.clip(jnp.exp(math.log(0.001) - 2.3025852 * jax.random.uniform(splits[8], (D, FF), jnp.float32) ** block_scale(splits[8], (D, FF), ((0, 8), (1, 4)), -0.2, 0.2)), 0.0001, 0.001)
    down_first = gaussian(splits[9], (FF, D), 0.002, 0.012, ((0, 4), (1, 8)), jnp.float32)
    down_second = jnp.clip(jnp.exp(math.log(0.001) - 2.3025852 * jax.random.uniform(splits[10], (FF, D), jnp.float32) ** block_scale(splits[10], (FF, D), ((0, 4), (1, 8)), -0.2, 0.2)), 0.0001, 0.001)
    return dict(tokens=tokens, targets=targets, norm_gain=norm_gain, up_master=up_master, down_master=down_master, up_probe=up_probe, down_probe=down_probe, up_first=up_first, up_second=up_second, down_first=down_first, down_second=down_second)


norm_eps = 1e-05
beta_one = 0.9
beta_two = 0.999
adam_eps = 1e-08

def signs_rows(probe):
    shifts = jnp.arange(32, dtype=jnp.int32)[:, None, None]
    bits = jnp.bitwise_and(jnp.right_shift(probe[None, :, :], shifts), 1)
    return (1 - 2 * bits).reshape(32 * probe.shape[0], probe.shape[1]).astype(jnp.bfloat16)

def signs_cols(probe):
    shifts = jnp.arange(32, dtype=jnp.int32)[None, :, None]
    bits = jnp.bitwise_and(jnp.right_shift(probe[:, None, :], shifts), 1)
    return (1 - 2 * bits).reshape(probe.shape[0], 32 * probe.shape[1]).astype(jnp.bfloat16)

def dot_first(left, right):
    return lax.dot_general(left, right, (((0,), (0,)), ((), ())), preferred_element_type=jnp.float32)

def dot_last(left, right):
    return lax.dot_general(left, right, (((1,), (1,)), ((), ())), preferred_element_type=jnp.float32)

def rounded(value):
    return lax.optimization_barrier(value.astype(jnp.bfloat16)).astype(jnp.float32)

def block_pass(rows, goal, norm_gain, up_weight, down_weight, up_signs, down_signs, tokens_all):
    values = rows.astype(jnp.float32)
    scale = lax.rsqrt(lax.optimization_barrier(jnp.mean(values * values, axis=-1, keepdims=True)) + norm_eps)
    normed = (values * scale * norm_gain).astype(jnp.bfloat16)
    preact = jnp.dot(normed, up_weight, preferred_element_type=jnp.float32)
    logistic = jax.nn.sigmoid(preact)
    active = (preact * logistic).astype(jnp.bfloat16)
    slopes = logistic * (1.0 + preact * (1.0 - logistic))
    curves = logistic * (1.0 - logistic) * (2.0 + preact * (1.0 - 2.0 * logistic))
    preact_dir = jnp.dot(normed, up_signs, preferred_element_type=jnp.float32)
    active_dir = (slopes * preact_dir).astype(jnp.bfloat16)
    output = jnp.dot(active, down_weight, preferred_element_type=jnp.float32)
    output_dir = jnp.dot(active_dir, down_weight, preferred_element_type=jnp.float32) + jnp.dot(active, down_signs, preferred_element_type=jnp.float32)
    diff = output - goal.astype(jnp.float32)
    residual = (diff / tokens_all).astype(jnp.bfloat16)
    residual_dir = (output_dir / tokens_all).astype(jnp.bfloat16)
    loss_part = 0.5 * jnp.sum(diff * diff) / tokens_all
    grad_active = dot_last(residual, down_weight)
    hess_active = dot_last(residual_dir, down_weight) + dot_last(residual, down_signs)
    grad_preact = (slopes * grad_active).astype(jnp.bfloat16)
    hess_preact = (curves * preact_dir * grad_active + slopes * hess_active).astype(jnp.bfloat16)
    up_grad = rounded(dot_first(normed, grad_preact))
    up_hess = rounded(dot_first(normed, hess_preact))
    down_grad = rounded(dot_first(active, residual))
    down_hess = rounded(dot_first(active, residual_dir) + dot_first(active_dir, residual))
    return (up_grad, up_hess, down_grad, down_hess, loss_part)

def moments(grad, hess, signs, first, second):
    hut = jnp.abs(signs.astype(jnp.float32) * hess)
    rows, cols = hut.shape
    means = lax.optimization_barrier(jnp.mean(hut.reshape(rows, cols // BLOCK, BLOCK), axis=-1))
    diag = jnp.repeat(means, BLOCK, axis=1)
    first_new = beta_one * first + (1.0 - beta_one) * grad
    second_new = beta_two * second + (1.0 - beta_two) * diag * diag
    direction = first_new / (1.0 - beta_one ** STEP) / (jnp.sqrt(second_new / (1.0 - beta_two ** STEP)) + adam_eps)
    return (first_new, second_new, direction)

def reference(tokens, targets, norm_gain, up_master, down_master, up_probe, down_probe, up_first, up_second, down_first, down_second):
    up_weight = up_master.astype(jnp.bfloat16)
    down_weight = down_master.astype(jnp.bfloat16)
    up_signs = signs_rows(up_probe)
    down_signs = signs_cols(down_probe)
    tokens_all = jnp.float32(TOKENS)
    blocks_in = tokens.reshape(N_DP, TOK_DEV, D)
    blocks_goal = targets.reshape(N_DP, TOK_DEV, D)

    def visit(carry, block):
        terms = block_pass(block[0], block[1], norm_gain, up_weight, down_weight, up_signs, down_signs, tokens_all)
        return (tuple((c + t for c, t in zip(carry, terms))), None)
    start = (jnp.zeros((D, FF), jnp.float32), jnp.zeros((D, FF), jnp.float32), jnp.zeros((FF, D), jnp.float32), jnp.zeros((FF, D), jnp.float32), jnp.zeros((), jnp.float32))
    totals, _ = lax.scan(visit, start, (blocks_in, blocks_goal))
    up_grad, up_hess, down_grad, down_hess, loss = totals
    up_moment, up_curvature, up_step = moments(up_grad, up_hess, up_signs, up_first, up_second)
    down_moment, down_curvature, down_step = moments(down_grad, down_hess, down_signs, down_first, down_second)
    return (loss, up_moment, up_curvature, up_step, down_moment, down_curvature, down_step)
```

```python
import jax
import jax.numpy as jnp
from jax import lax
from jax.experimental import pallas as pl
from jax.experimental.pallas import tpu as pltpu
from jax.sharding import PartitionSpec as P

BLOCK = 16
STEP = 10


norm_eps = 1e-05
beta_one = 0.9
beta_two = 0.999
adam_eps = 1e-08


def signs_kernel(probe_ref, out_ref):
    bits = lax.shift_right_logical(probe_ref[...], pl.program_id(0)) & 1
    out_ref[...] = (1 - 2 * bits).astype(jnp.float32).astype(jnp.bfloat16)


def signs_rows(probe):
    rows, cols = probe.shape
    return pl.pallas_call(
        signs_kernel,
        grid=(32,),
        in_specs=[pl.BlockSpec((rows, cols), lambda bit: (0, 0))],
        out_specs=pl.BlockSpec((rows, cols), lambda bit: (bit, 0)),
        out_shape=jax.ShapeDtypeStruct((32 * rows, cols), jnp.bfloat16),
        cost_estimate=pl.CostEstimate(
            flops=32 * 256 * rows * cols, bytes_accessed=64 * rows * cols, transcendentals=0
        ),
    )(probe)


def dot_first(left, right):
    return lax.dot_general(
        left, right, (((0,), (0,)), ((), ())), preferred_element_type=jnp.float32
    )


def block_means(values):
    cols = values.shape[1]
    row = lax.broadcasted_iota(jnp.int32, (cols, cols), 0) // BLOCK
    col = lax.broadcasted_iota(jnp.int32, (cols, cols), 1) // BLOCK
    same = (row == col).astype(jnp.bfloat16)
    return jnp.dot(values.astype(jnp.bfloat16), same, preferred_element_type=jnp.float32) / BLOCK


def dot_last(left, right):
    return lax.dot_general(
        left, right, (((1,), (1,)), ((), ())), preferred_element_type=jnp.float32
    )


def moments(grad, hess, signs, first, second):
    diag = block_means(jnp.abs(signs * hess))
    first_new = beta_one * first + (1.0 - beta_one) * grad
    second_new = beta_two * second + (1.0 - beta_two) * diag * diag
    direction = (
        first_new
        / (1.0 - beta_one**STEP)
        / (jnp.sqrt(second_new / (1.0 - beta_two**STEP)) + adam_eps)
    )
    return (first_new, second_new, direction)


def sum_over_fsdp(value):
    parts = lax.axis_size("fsdp")
    rows, cols = value.shape
    blocks = value.reshape(parts, rows // parts, cols)
    terms = lax.all_to_all(blocks, "fsdp", split_axis=0, concat_axis=0)
    total = jnp.sum(terms.astype(jnp.float32), axis=0).astype(jnp.bfloat16)
    copies = jnp.broadcast_to(total[None], blocks.shape)
    everyone = lax.all_to_all(copies, "fsdp", split_axis=0, concat_axis=0)
    return everyone.reshape(rows, cols).astype(jnp.float32)


def local(
    tokens,
    targets,
    norm_gain,
    up_master,
    down_master,
    up_probe,
    down_probe,
    up_first,
    up_second,
    down_first,
    down_second,
):
    tok_rows = tokens.shape[0]
    tokens_all = jnp.float32(tok_rows * lax.axis_size("dp"))
    shares = lax.axis_size("dp")
    hidden = up_master.shape[1]
    own_rows = up_master.shape[0]
    values = tokens.astype(jnp.float32)
    scale = lax.rsqrt(jnp.mean(values * values, axis=-1, keepdims=True) + norm_eps)
    normed = (values * scale * norm_gain).astype(jnp.bfloat16)
    owned_in = lax.all_to_all(normed, "dp", split_axis=1, concat_axis=0, tiled=True)
    down_full = lax.all_gather(down_master.astype(jnp.bfloat16), "dp", axis=1, tiled=True)
    partial_pre = jnp.dot(
        owned_in, up_master.astype(jnp.bfloat16), preferred_element_type=jnp.float32
    ).astype(jnp.bfloat16)
    pieces = lax.all_to_all(
        partial_pre.reshape(shares, tok_rows, hidden), "dp", split_axis=0, concat_axis=0
    )
    up_signs = signs_rows(up_probe)
    down_signs_t = signs_rows(down_probe.T)
    preact_dir = jnp.dot(normed, up_signs, preferred_element_type=jnp.float32)
    preact = jnp.sum(pieces.astype(jnp.float32), axis=0)
    logistic = jax.nn.sigmoid(preact)
    active = (preact * logistic).astype(jnp.bfloat16)
    slopes = logistic * (1.0 + preact * (1.0 - logistic))
    curves = logistic * (1.0 - logistic) * (2.0 + preact * (1.0 - 2.0 * logistic))
    active_dir = (slopes * preact_dir).astype(jnp.bfloat16)
    partial_value = jnp.dot(active, down_full, preferred_element_type=jnp.float32)
    partial_dir = jnp.dot(active_dir, down_full, preferred_element_type=jnp.float32) + dot_last(
        active, down_signs_t
    )
    hidden_forward = lax.all_gather(jnp.stack([active, active_dir]), "dp", axis=0)
    output = sum_over_fsdp(partial_value.astype(jnp.bfloat16))
    output_dir = sum_over_fsdp(partial_dir.astype(jnp.bfloat16))
    diff = output - targets.astype(jnp.float32)
    residual = (diff / tokens_all).astype(jnp.bfloat16)
    residual_dir = (output_dir / tokens_all).astype(jnp.bfloat16)
    loss = lax.psum(0.5 * jnp.sum(diff * diff) / tokens_all, "dp")
    grad_active = dot_last(residual, down_full)
    hess_active = dot_last(residual_dir, down_full) + jnp.dot(
        residual, down_signs_t, preferred_element_type=jnp.float32
    )
    grad_preact = (slopes * grad_active).astype(jnp.bfloat16)
    hess_preact = (curves * preact_dir * grad_active + slopes * hess_active).astype(jnp.bfloat16)
    hidden_backward = lax.all_gather(jnp.stack([grad_preact, hess_preact]), "dp", axis=0)
    owned_res = lax.all_to_all(residual, "dp", split_axis=1, concat_axis=0, tiled=True)
    owned_dir = lax.all_to_all(residual_dir, "dp", split_axis=1, concat_axis=0, tiled=True)
    act_all = hidden_forward[:, 0].reshape(shares * tok_rows, hidden)
    actdir_all = hidden_forward[:, 1].reshape(shares * tok_rows, hidden)
    grad_all = hidden_backward[:, 0].reshape(shares * tok_rows, hidden)
    hess_all = hidden_backward[:, 1].reshape(shares * tok_rows, hidden)
    down_grad = dot_first(act_all, owned_res)
    down_hess = dot_first(act_all, owned_dir) + dot_first(actdir_all, owned_res)
    up_grad = dot_first(owned_in, grad_all)
    up_hess = dot_first(owned_in, hess_all)
    offset = lax.axis_index("dp") * own_rows
    up_own = lax.dynamic_slice_in_dim(up_signs, offset, own_rows, 0).astype(jnp.float32)
    down_own = lax.dynamic_slice_in_dim(down_signs_t, offset, own_rows, 0).T.astype(jnp.float32)
    up_moment, up_curvature, up_step = moments(up_grad, up_hess, up_own, up_first, up_second)
    down_moment, down_curvature, down_step = moments(
        down_grad, down_hess, down_own, down_first, down_second
    )
    return (loss, up_moment, up_curvature, up_step, down_moment, down_curvature, down_step)


def solution(mesh):
    placed = (
        P("dp", None),
        P("dp", None),
        P(),
        P("dp", "fsdp"),
        P("fsdp", "dp"),
        P(None, "fsdp"),
        P("fsdp", None),
        P("dp", "fsdp"),
        P("dp", "fsdp"),
        P("fsdp", "dp"),
        P("fsdp", "dp"),
    )
    return jax.shard_map(
        local,
        mesh=mesh,
        in_specs=placed,
        out_specs=(
            P(),
            P("dp", "fsdp"),
            P("dp", "fsdp"),
            P("dp", "fsdp"),
            P("fsdp", "dp"),
            P("fsdp", "dp"),
            P("fsdp", "dp"),
        ),
        check_vma=False,
    )
```
